32 devices in a mesh: dp: 16 (over z, x, core), tensor: 2 (over y).
Axes of the slice: x: 2, y: 2, z: 4, core: 2. Of those that a mesh axis runs over, the one named last changes fastest.
Arguments:
- tokens: bfloat16 [8192, 768], P(('dp', 'tensor')), may hold values from -6 to 6
- cotangent: bfloat16 [8192, 768], P(('dp', 'tensor')), may hold values from -6 to 6
- block_seq: int32 [64], P('dp'), may hold values from 0 to 3, as said below
- block_fill: int32 [64], P('dp'), may hold values from 1 to 128, as said below
- qkv_weight: bfloat16 [3, 768, 768], P(None, 'dp', 'tensor'), may hold values from -2 to 2
- out_weight: bfloat16 [768, 768], P('tensor', 'dp'), may hold values from -0.875 to 0.875
- in_weight: bfloat16 [2, 768, 1152], P(None, 'dp', 'tensor'), may hold values from -0.21875 to 0.21875
- down_weight: bfloat16 [1152, 768], P('tensor', 'dp'), may hold values from -0.1875 to 0.1875
- norm1_gain: bfloat16 [768], P('dp'), may hold values from 0.099609375 to 1.8984375
- norm2_gain: bfloat16 [768], P('dp'), may hold values from 0.099609375 to 1.8984375
Outputs:
- output: bfloat16 [8192, 768], P(('dp', 'tensor'))
- input_grad: bfloat16 [8192, 768], P(('dp', 'tensor'))
- joined_grad: float32 [3, 768, 768], P(None, 'dp', 'tensor')
- out_proj_grad: float32 [768, 768], P('tensor', 'dp')
- in_grad: float32 [2, 768, 1152], P(None, 'dp', 'tensor')
- down_grad: float32 [1152, 768], P('tensor', 'dp')
- norm1_grad: float32 [768], P('dp')
- norm2_grad: float32 [768], P('dp')
The draws below stay inside these ranges and needn't reach their ends.
Inputs may be any that keep to these rules, and one draw needn't show every extreme that they name: `block_seq`: on each index of dp, the numbers of its 4 blocks in order: 0 for the first, then equal to or one more than the number before; blocks with one number form one sequence. `block_fill`: 128 in every block but the last of its sequence.
All inputs are finite; a program needn't handle non-finite values.
Results may differ from the reference program's by a relative error of at most 0.012.
The reference program's roundings to bfloat16 on the way count: a program that leaves them out, or rounds other values in their place, can miss the bound.
Values may be sent and summed in bfloat16 or wider, within the bound.
No kernel may reach another device: no remote copies, remote signals or barrier semaphores. Data moves between devices by JAX's collectives and lax.ppermute only.
A program may use at most 128 MiB of HBM per device.

```python
import math
import jax
import jax.numpy as jnp
from jax import lax

D = 768
H = 12
FF = 1152
BLK = 128
ROWS_DEV = 512
HD = 64
ROWS = 8192
NBLK = 64


def block_plan(key):
    folded = jax.random.fold_in(key, 7)
    start_key, fill_key = jax.random.split(folded)
    per_group = ROWS_DEV // BLK
    group_count = NBLK // per_group
    starts = jax.random.randint(start_key, (group_count, per_group), 0, 2)
    first_group = (jnp.arange(group_count, dtype=jnp.int32) == 0)[:, None]
    starts = jnp.where(first_group, 1, starts)
    starts = jnp.concatenate([jnp.ones((group_count, 1), jnp.int32), starts[:, 1:]], axis=1)
    numbers = jnp.cumsum(starts, axis=1) - 1
    closing = jnp.concatenate([starts[:, 1:], jnp.ones((group_count, 1), jnp.int32)], axis=1)
    partial_fill = jax.random.randint(fill_key, (group_count, per_group), 1, BLK + 1)
    fill_counts = jnp.where(closing == 1, partial_fill, BLK)
    return (numbers.reshape(-1).astype(jnp.int32), fill_counts.reshape(-1).astype(jnp.int32))


def draw_block_seq(key, part):
    return block_plan(key)[0]


def draw_block_fill(key, part):
    return block_plan(key)[1]


def draw_qkv_weight(key, part):
    base_key = jax.random.fold_in(key, 0)
    spread = 1.0 / math.sqrt(D)
    drawn = jnp.clip(jax.random.normal(base_key, (3, D, D), jnp.float32), -6.0, 6.0) * spread
    return drawn.astype(jnp.bfloat16)


def with_spikes(values, rng, source, target, shards_of, factor):
    def block_of(dim):
        return (jnp.arange(values.shape[dim]) // (values.shape[dim] // shards_of)).reshape((-1,) + (1,) * (values.ndim - 1 - dim))

    one_side = jax.random.permutation(rng, shards_of)[block_of(target)]
    other_side = (block_of(target) + shards_of // 2) % shards_of
    return jnp.where((block_of(source) == one_side) | (block_of(source) == other_side), factor * values, values)


def levels(key, extent, shards, smallest, high):
    loudness, own = 1.0, jax.random.fold_in(key, 6)
    for dim, parts in shards:
        draws = jnp.exp(jax.random.uniform(jax.random.fold_in(own, dim), (parts,), jnp.float32, smallest / len(shards), high / len(shards)))
        loudness = loudness * jnp.repeat(draws, extent[dim] // parts).reshape([-1 if axis == dim else 1 for axis in range(len(extent))])
    return loudness


def noise(own_key, extent, scale, most, cuts=(), kind=jnp.bfloat16):
    array = jax.random.normal(own_key, extent, jnp.float32) * scale
    if len(cuts) > 0:
        array = levels(own_key, extent, cuts, -0.22, 0.18) * array
    return jnp.clip(array, min=-most, max=most).astype(kind)


def noise_with(rng, shape, deviation, reach, cuts, heavy, held_as=jnp.bfloat16):
    values = deviation * jax.random.normal(rng, shape, jnp.float32)
    if cuts:
        values = values * levels(rng, shape, cuts, -0.22, 0.18)
    return jnp.clip(with_spikes(values, jax.random.fold_in(rng, 3), *heavy), -reach, reach).astype(held_as)


def setup_inputs(seed: int = 0) -> dict:
    arg_keys = jax.random.split(jax.random.key(seed), 11)
    tokens = noise_with(arg_keys[0], (ROWS, D), 1.0, 6.0, ((0, 32),), (0, 1, 32, 2.75))
    cotangent = noise_with(arg_keys[1], (ROWS, D), 1.0, 6.0, ((0, 32),), (0, 1, 32, 2.75))
    block_seq = draw_block_seq(jax.random.fold_in(arg_keys[10], 71), 0)
    block_fill = draw_block_fill(jax.random.fold_in(arg_keys[10], 71), 0)
    qkv_weight = draw_qkv_weight(jax.random.fold_in(arg_keys[10], 71), 0)
    out_weight = noise(arg_keys[5], (D, D), (D // 16) ** -0.5, 0.875, ((0, 2), (1, 16)))
    in_weight = noise(arg_keys[6], (2, D, FF), D ** -0.5, 0.21875, ((1, 16), (2, 2)))
    down_weight = noise(arg_keys[7], (FF, D), FF ** -0.5, 0.1875, ((0, 2), (1, 16)))
    norm1_gain = jnp.clip(1.0 + 0.18 * jax.random.normal(arg_keys[8], (D,), jnp.float32), 0.099609375, 1.8984375).astype(jnp.bfloat16)
    norm2_gain = jnp.clip(1.0 + 0.18 * jax.random.normal(arg_keys[9], (D,), jnp.float32), 0.099609375, 1.8984375).astype(jnp.bfloat16)
    return dict(tokens=tokens, cotangent=cotangent, block_seq=block_seq, block_fill=block_fill, qkv_weight=qkv_weight, out_weight=out_weight, in_weight=in_weight, down_weight=down_weight, norm1_gain=norm1_gain, norm2_gain=norm2_gain)


epsilon = 1e-05
rope_base = 160000.0
big_negative = -1e+30

def narrow(values):
    return lax.optimization_barrier(values.astype(jnp.bfloat16))

def block_size(row_count):
    if row_count % 512 == 0:
        return 512
    return row_count

def layer_stats(values):
    centre = values - lax.optimization_barrier(jnp.mean(values, axis=-1, keepdims=True))
    inv_std = lax.rsqrt(lax.optimization_barrier(jnp.mean(centre * centre, axis=-1, keepdims=True)) + epsilon)
    return (centre * inv_std, inv_std)

def layer_back(grad_normed, normed, inv_std):
    mean_grad = lax.optimization_barrier(jnp.mean(grad_normed, axis=-1, keepdims=True))
    mean_cross = lax.optimization_barrier(jnp.mean(grad_normed * normed, axis=-1, keepdims=True))
    return inv_std * (grad_normed - mean_grad - normed * mean_cross)

def gelu_parts(values):
    normal_cdf = 0.5 * (1.0 + jax.scipy.special.erf(values * (1.0 / math.sqrt(2.0))))
    density = jnp.exp(-0.5 * values * values) * (1.0 / math.sqrt(2.0 * math.pi))
    return (values * normal_cdf, normal_cdf + values * density)

def block_layout(seq_ids, fill_counts):
    block_count = seq_ids.shape[0]
    block_order = jnp.arange(block_count, dtype=jnp.int32)
    same_seq = seq_ids[:, None] == seq_ids[None, :]
    first_block = lax.optimization_barrier(jnp.min(jnp.where(same_seq, block_order[None, :], block_count), axis=1)).astype(jnp.int32)
    offsets = jnp.arange(BLK, dtype=jnp.int32)
    position = ((block_order - first_block)[:, None] * BLK + offsets[None, :]).reshape(-1)
    real_key = (offsets[None, :] < fill_counts[:, None]).reshape(-1)
    token_seq = jnp.repeat(seq_ids, BLK)
    allowed = (token_seq[:, None] == token_seq[None, :]) & real_key[None, :]
    return (position, allowed)

def rope_tables(position):
    half_dim = HD // 2
    frequency = rope_base ** (-jnp.arange(half_dim, dtype=jnp.float32) * (2.0 / HD))
    angles = position.astype(jnp.float32)[:, None] * frequency[None, :]
    cosine = jnp.concatenate([jnp.cos(angles), jnp.cos(angles)], axis=1)
    sine_table = jnp.concatenate([jnp.sin(angles), jnp.sin(angles)], axis=1)
    return (cosine[:, None, :], sine_table[:, None, :])

def rotate_half(values):
    half_dim = values.shape[-1] // 2
    return jnp.concatenate([-values[..., half_dim:], values[..., :half_dim]], axis=-1)

def rope_apply(values, cosine, sine_table):
    return values * cosine + rotate_half(values) * sine_table

def rope_back(grad_heads, cosine, sine_table):
    return grad_heads * cosine - rotate_half(grad_heads * sine_table)

def attend_forward(queries, key_heads, values, allowed):
    row_count = key_heads.shape[0]
    block_rows = block_size(row_count)
    blocks = row_count // block_rows
    score_scale = 1.0 / math.sqrt(HD)
    query_blocks = queries.reshape(blocks, block_rows, queries.shape[1], queries.shape[2])
    mask_blocks = allowed.reshape(blocks, block_rows, row_count)
    key_float = key_heads.astype(jnp.float32)
    value_float = values.astype(jnp.float32)

    def one_block(pieces):
        query_block, mask_block = pieces
        scores = jnp.einsum('qhd,khd->hqk', query_block.astype(jnp.float32), key_float) * score_scale
        scores = jnp.where(mask_block[None], scores, big_negative)
        row_peak = lax.optimization_barrier(jnp.max(scores, axis=-1, keepdims=True))
        log_total = row_peak + jnp.log(lax.optimization_barrier(jnp.sum(jnp.exp(scores - row_peak), axis=-1, keepdims=True)))
        weights = narrow(jnp.exp(scores - log_total))
        mixed_rows = narrow(jnp.einsum('hqk,khd->qhd', weights.astype(jnp.float32), value_float))
        return (mixed_rows, log_total[..., 0])
    mixed_heads, log_total = lax.map(one_block, (query_blocks, mask_blocks))
    return (mixed_heads.reshape(queries.shape), log_total)

def attend_backward(queries, key_heads, values, allowed, log_total, mixed_heads, grad_mixed):
    row_count = key_heads.shape[0]
    block_rows = block_size(row_count)
    blocks = row_count // block_rows
    score_scale = 1.0 / math.sqrt(HD)
    block_shape = (blocks, block_rows, queries.shape[1], queries.shape[2])
    key_float = key_heads.astype(jnp.float32)
    value_float = values.astype(jnp.float32)
    pieces = (queries.reshape(block_shape), allowed.reshape(blocks, block_rows, row_count), log_total, mixed_heads.reshape(block_shape), grad_mixed.reshape(block_shape))

    def one_block(running, piece_set):
        grad_keys, grad_values = running
        query_block, mask_block, log_block, mixed_block, grad_block = piece_set
        query_float = query_block.astype(jnp.float32)
        grad_float = grad_block.astype(jnp.float32)
        scores = jnp.einsum('qhd,khd->hqk', query_float, key_float) * score_scale
        scores = jnp.where(mask_block[None], scores, big_negative)
        prob_rows = jnp.exp(scores - log_block[..., None])
        prob_narrow = narrow(prob_rows)
        grad_values = grad_values + jnp.einsum('hqk,qhd->khd', prob_narrow.astype(jnp.float32), grad_float)
        grad_probs = jnp.einsum('qhd,khd->hqk', grad_float, value_float)
        delta_rows = jnp.einsum('qhd,qhd->hq', grad_float, mixed_block.astype(jnp.float32))
        grad_scores = narrow(prob_rows * (grad_probs - delta_rows[..., None]) * score_scale)
        grad_scores_float = grad_scores.astype(jnp.float32)
        grad_query = jnp.einsum('hqk,khd->qhd', grad_scores_float, key_float)
        grad_keys = grad_keys + jnp.einsum('hqk,qhd->khd', grad_scores_float, query_float)
        return ((grad_keys, grad_values), grad_query)
    zero_heads = jnp.zeros(key_heads.shape, jnp.float32)
    (grad_keys, grad_values), grad_query = lax.scan(one_block, (zero_heads, zero_heads), pieces)
    return (grad_query.reshape(queries.shape), grad_keys, grad_values)

def one_group(tokens, cotangent, seq_ids, fill_counts, qkv_weight, out_weight, in_weight, down_weight, norm1_gain, norm2_gain):
    row_count = tokens.shape[0]
    heads_shape = (row_count, H, HD)
    position, allowed = block_layout(seq_ids, fill_counts)
    cosine, sine_table = rope_tables(position)
    tokens_float = tokens.astype(jnp.float32)
    normed_one, inv_one = layer_stats(tokens_float)
    hidden_one = narrow(normed_one * norm1_gain.astype(jnp.float32))
    projected = [jnp.dot(hidden_one, qkv_weight[which], preferred_element_type=jnp.float32).reshape(heads_shape) for which in range(3)]
    queries = narrow(rope_apply(projected[0], cosine, sine_table))
    key_heads = narrow(rope_apply(projected[1], cosine, sine_table))
    values = narrow(projected[2])
    mixed_heads, log_total = attend_forward(queries, key_heads, values, allowed)
    mixed_flat = mixed_heads.reshape(row_count, D)
    resid_two = tokens_float + jnp.dot(mixed_flat, out_weight, preferred_element_type=jnp.float32)
    normed_two, inv_two = layer_stats(resid_two)
    hidden_two = narrow(normed_two * norm2_gain.astype(jnp.float32))
    act_pre = jnp.dot(hidden_two, in_weight[0], preferred_element_type=jnp.float32)
    linear = jnp.dot(hidden_two, in_weight[1], preferred_element_type=jnp.float32)
    gelu_value, gelu_slope = gelu_parts(act_pre)
    inner_act = narrow(gelu_value * linear)
    output = (resid_two + jnp.dot(inner_act, down_weight, preferred_element_type=jnp.float32)).astype(jnp.bfloat16)
    down_grad = jnp.dot(inner_act.T, cotangent, preferred_element_type=jnp.float32)
    grad_inner = jnp.dot(cotangent, down_weight.T, preferred_element_type=jnp.float32)
    grad_act = narrow(grad_inner * linear * gelu_slope)
    grad_linear = narrow(grad_inner * gelu_value)
    in_grad = jnp.stack([jnp.dot(hidden_two.T, grad_act, preferred_element_type=jnp.float32), jnp.dot(hidden_two.T, grad_linear, preferred_element_type=jnp.float32)])
    grad_hidden_two = jnp.dot(grad_act, in_weight[0].T, preferred_element_type=jnp.float32) + jnp.dot(grad_linear, in_weight[1].T, preferred_element_type=jnp.float32)
    norm2_grad = lax.optimization_barrier(jnp.sum(grad_hidden_two * normed_two, axis=0))
    grad_resid = cotangent.astype(jnp.float32) + layer_back(grad_hidden_two * norm2_gain.astype(jnp.float32), normed_two, inv_two)
    grad_resid_b = narrow(grad_resid)
    out_proj_grad = jnp.dot(mixed_flat.T, grad_resid_b, preferred_element_type=jnp.float32)
    grad_mixed = narrow(jnp.dot(grad_resid_b, out_weight.T, preferred_element_type=jnp.float32)).reshape(heads_shape)
    grad_query, grad_keys, grad_values = attend_backward(queries, key_heads, values, allowed, log_total, mixed_heads, grad_mixed)
    grad_joined = narrow(jnp.stack([rope_back(grad_query, cosine, sine_table).reshape(row_count, D), rope_back(grad_keys, cosine, sine_table).reshape(row_count, D), grad_values.reshape(row_count, D)]))
    joined_grad = jnp.stack([jnp.dot(hidden_one.T, grad_joined[which], preferred_element_type=jnp.float32) for which in range(3)])
    grad_hidden_one = jnp.dot(grad_joined[0], qkv_weight[0].T, preferred_element_type=jnp.float32)
    grad_hidden_one = grad_hidden_one + jnp.dot(grad_joined[1], qkv_weight[1].T, preferred_element_type=jnp.float32)
    grad_hidden_one = grad_hidden_one + jnp.dot(grad_joined[2], qkv_weight[2].T, preferred_element_type=jnp.float32)
    norm1_grad = lax.optimization_barrier(jnp.sum(grad_hidden_one * normed_one, axis=0))
    input_grad = (grad_resid + layer_back(grad_hidden_one * norm1_gain.astype(jnp.float32), normed_one, inv_one)).astype(jnp.bfloat16)
    return (output, input_grad, (joined_grad, out_proj_grad, in_grad, down_grad, norm1_grad, norm2_grad))

def reference(tokens, cotangent, block_seq, block_fill, qkv_weight, out_weight, in_weight, down_weight, norm1_gain, norm2_gain):
    group_count = tokens.shape[0] // ROWS_DEV
    per_group = ROWS_DEV // BLK
    inputs = (tokens.reshape(group_count, ROWS_DEV, D), cotangent.reshape(group_count, ROWS_DEV, D), block_seq.reshape(group_count, per_group), block_fill.reshape(group_count, per_group))

    def scan_step(totals, pieces):
        output, input_grad, grads = one_group(pieces[0], pieces[1], pieces[2], pieces[3], qkv_weight, out_weight, in_weight, down_weight, norm1_gain, norm2_gain)
        return (jax.tree.map(jnp.add, totals, grads), (output, input_grad))
    zero_grads = (jnp.zeros((3, D, D), jnp.float32), jnp.zeros((D, D), jnp.float32), jnp.zeros((2, D, FF), jnp.float32), jnp.zeros((FF, D), jnp.float32), jnp.zeros((D,), jnp.float32), jnp.zeros((D,), jnp.float32))
    totals, (outputs, input_grads) = lax.scan(scan_step, zero_grads, inputs)
    return (outputs.reshape(group_count * ROWS_DEV, D), input_grads.reshape(group_count * ROWS_DEV, D), totals[0], totals[1], totals[2], totals[3], totals[4], totals[5])
```

```python
import functools
import math

import jax
import jax.numpy as jnp
from jax import lax
from jax.experimental import pallas as pl
from jax.experimental.pallas import tpu as pltpu
from jax.sharding import PartitionSpec as P

BLK = 128
HD = 64


epsilon = 1e-05
rope_base = 160000.0
big_negative = -1e30


def layer_stats(values):
    centre = values - jnp.mean(values, axis=-1, keepdims=True)
    inv_std = lax.rsqrt(jnp.mean(centre * centre, axis=-1, keepdims=True) + epsilon)
    return (centre * inv_std, inv_std)


def layer_back(grad_normed, normed, inv_std):
    mean_grad = jnp.mean(grad_normed, axis=-1, keepdims=True)
    mean_cross = jnp.mean(grad_normed * normed, axis=-1, keepdims=True)
    return inv_std * (grad_normed - mean_grad - normed * mean_cross)


def gelu_parts(values):
    normal_cdf = 0.5 * (1.0 + jax.scipy.special.erf(values * (1.0 / math.sqrt(2.0))))
    density = jnp.exp(-0.5 * values * values) * (1.0 / math.sqrt(2.0 * math.pi))
    return (values * normal_cdf, normal_cdf + values * density)


def block_layout(seq_ids, fill_counts):
    block_count = seq_ids.shape[0]
    block_order = jnp.arange(block_count, dtype=jnp.int32)
    same_seq = seq_ids[:, None] == seq_ids[None, :]
    first_block = jnp.min(jnp.where(same_seq, block_order[None, :], block_count), axis=1)
    offsets = jnp.arange(BLK, dtype=jnp.int32)
    position = ((block_order - first_block)[:, None] * BLK + offsets[None, :]).reshape(-1)
    real_key = (offsets[None, :] < fill_counts[:, None]).reshape(-1)
    token_seq = jnp.repeat(seq_ids, BLK)
    allowed = (token_seq[:, None] == token_seq[None, :]) & real_key[None, :]
    return (position, allowed)


def rope_tables(position):
    half_dim = HD // 2
    frequency = rope_base ** (-jnp.arange(half_dim, dtype=jnp.float32) * (2.0 / HD))
    angles = position.astype(jnp.float32)[:, None] * frequency[None, :]
    cosine = jnp.concatenate([jnp.cos(angles), jnp.cos(angles)], axis=1)
    sine_table = jnp.concatenate([jnp.sin(angles), jnp.sin(angles)], axis=1)
    return (cosine[:, None, :], sine_table[:, None, :])


def rotate_half(values):
    half_dim = values.shape[-1] // 2
    return jnp.concatenate([-values[..., half_dim:], values[..., :half_dim]], axis=-1)


def rope_apply(values, cosine, sine_table):
    return values * cosine + rotate_half(values) * sine_table


def rope_back(grad_heads, cosine, sine_table):
    return grad_heads * cosine - rotate_half(grad_heads * sine_table)


def attend_forward(queries, key_heads, values, allowed):
    row_count = key_heads.shape[0]
    block_rows = row_count
    blocks = row_count // block_rows
    score_scale = 1.0 / math.sqrt(HD)
    query_blocks = queries.reshape(blocks, block_rows, queries.shape[1], queries.shape[2])
    mask_blocks = allowed.reshape(blocks, block_rows, row_count)

    def one_block(pieces):
        query_block, mask_block = pieces
        scores = (
            jnp.einsum("qhd,khd->hqk", query_block, key_heads, preferred_element_type=jnp.float32)
            * score_scale
        )
        scores = jnp.where(mask_block[None], scores, big_negative)
        row_peak = jnp.max(scores, axis=-1, keepdims=True)
        log_total = row_peak + jnp.log(jnp.sum(jnp.exp(scores - row_peak), axis=-1, keepdims=True))
        weights = jnp.exp(scores - log_total).astype(jnp.bfloat16)
        mixed_rows = jnp.einsum(
            "hqk,khd->qhd", weights, values, preferred_element_type=jnp.float32
        ).astype(jnp.bfloat16)
        return (mixed_rows, log_total[..., 0])

    mixed_heads, log_total = lax.map(one_block, (query_blocks, mask_blocks))
    return (mixed_heads.reshape(queries.shape), log_total)


def attend_backward(queries, key_heads, values, allowed, log_total, mixed_heads, grad_mixed):
    row_count = key_heads.shape[0]
    block_rows = row_count
    blocks = row_count // block_rows
    score_scale = 1.0 / math.sqrt(HD)
    block_shape = (blocks, block_rows, queries.shape[1], queries.shape[2])
    pieces = (
        queries.reshape(block_shape),
        allowed.reshape(blocks, block_rows, row_count),
        log_total,
        mixed_heads.reshape(block_shape),
        grad_mixed.reshape(block_shape),
    )

    def one_block(running, piece_set):
        grad_keys, grad_values = running
        query_block, mask_block, log_block, mixed_block, grad_block = piece_set
        scores = (
            jnp.einsum("qhd,khd->hqk", query_block, key_heads, preferred_element_type=jnp.float32)
            * score_scale
        )
        scores = jnp.where(mask_block[None], scores, big_negative)
        prob_rows = jnp.exp(scores - log_block[..., None])
        grad_values = grad_values + jnp.einsum(
            "hqk,qhd->khd",
            prob_rows.astype(jnp.bfloat16),
            grad_block,
            preferred_element_type=jnp.float32,
        )
        grad_probs = jnp.einsum(
            "qhd,khd->hqk", grad_block, values, preferred_element_type=jnp.float32
        )
        delta_rows = jnp.einsum(
            "qhd,qhd->hq", grad_block, mixed_block, preferred_element_type=jnp.float32
        )
        grad_scores = (prob_rows * (grad_probs - delta_rows[..., None]) * score_scale).astype(
            jnp.bfloat16
        )
        grad_query = jnp.einsum(
            "hqk,khd->qhd", grad_scores, key_heads, preferred_element_type=jnp.float32
        )
        grad_keys = grad_keys + jnp.einsum(
            "hqk,qhd->khd", grad_scores, query_block, preferred_element_type=jnp.float32
        )
        return ((grad_keys, grad_values), grad_query)

    zero_heads = jnp.zeros(key_heads.shape, jnp.float32)
    (grad_keys, grad_values), grad_query = lax.scan(one_block, (zero_heads, zero_heads), pieces)
    return (grad_query.reshape(queries.shape), grad_keys, grad_values)


def swap_dp(values, bit):
    count = lax.axis_size("dp")
    return lax.ppermute(values, "dp", [(i, i ^ (1 << bit)) for i in range(count)])


def swap_tensor(values):
    count = lax.axis_size("tensor")
    return lax.ppermute(values, "tensor", [(i, (i + 1) % count) for i in range(count)])


def gather_blocks(shard, order):
    held = shard[None]
    for bit in order:
        held = jnp.concatenate([held, swap_dp(held, bit)], axis=0)
    return held


def slot_blocks(order):
    slots = [0]
    for bit in order:
        slots = slots + [s | (1 << bit) for s in slots]
    return slots


def canonical(held, order, mine):
    slots = slot_blocks(order)
    where = [0] * len(slots)
    for slot, block in enumerate(slots):
        where[block] = slot
    table = jnp.asarray(where, jnp.int32)[jnp.arange(len(slots), dtype=jnp.int32) ^ mine]

    def kernel(table_ref, in_ref, out_ref):
        out_ref[...] = in_ref[...]

    block = (1,) + held.shape[1:]
    zeros = (0,) * (held.ndim - 1)
    return pl.pallas_call(
        kernel,
        grid_spec=pltpu.PrefetchScalarGridSpec(
            num_scalar_prefetch=1,
            grid=(len(slots),),
            in_specs=[pl.BlockSpec(block, lambda i, t: (t[i],) + zeros)],
            out_specs=pl.BlockSpec(block, lambda i, t: (i,) + zeros),
        ),
        out_shape=jax.ShapeDtypeStruct(held.shape, held.dtype),
    )(table, held)


def relative(blocks, mine):
    table = jnp.arange(blocks.shape[0], dtype=jnp.int32) ^ mine

    def kernel(table_ref, in_ref, out_ref):
        out_ref[...] = in_ref[...]

    block = (1,) + blocks.shape[1:]
    zeros = (0,) * (blocks.ndim - 1)
    return pl.pallas_call(
        kernel,
        grid_spec=pltpu.PrefetchScalarGridSpec(
            num_scalar_prefetch=1,
            grid=(blocks.shape[0],),
            in_specs=[pl.BlockSpec(block, lambda i, t: (t[i],) + zeros)],
            out_specs=pl.BlockSpec(block, lambda i, t: (i,) + zeros),
        ),
        out_shape=jax.ShapeDtypeStruct(blocks.shape, blocks.dtype),
    )(table, blocks)


def scatter_sum(slots):
    count = slots.shape[0]
    bit = 0
    while count > 1:
        pairs = slots.reshape((count // 2, 2) + slots.shape[1:])
        arrived = swap_dp(pairs[:, 1].astype(jnp.bfloat16), bit)
        slots = pairs[:, 0] + arrived.astype(jnp.float32)
        count //= 2
        bit += 1
    return slots[0]


def sum_all(values):
    values = values + swap_tensor(values)
    count = lax.axis_size("dp")
    bit = 0
    while (1 << bit) < count:
        values = values + swap_dp(values, bit)
        bit += 1
    return values


def local(
    tokens,
    cotangent,
    block_seq,
    block_fill,
    qkv_weight,
    out_weight,
    in_weight,
    down_weight,
    norm1_gain,
    norm2_gain,
):
    mine = lax.axis_index("dp")
    half = lax.axis_index("tensor")
    dp = lax.axis_size("dp")
    bits = dp.bit_length() - 1
    order = list(range(bits - 1, -1, -1))
    sub = qkv_weight.shape[1]
    wide = qkv_weight.shape[2]
    units = in_weight.shape[2]
    rows = tokens.shape[0]
    width = tokens.shape[1]

    gains = jnp.stack([norm1_gain, norm2_gain])
    gains = jnp.pad(gains, ((0, 14), (0, wide - sub)))
    attn_shard = jnp.concatenate([qkv_weight.reshape(3 * sub, wide), gains], axis=0)
    out_mine = out_weight.T
    out_other = swap_tensor(out_mine)
    ffn_shard = jnp.concatenate([in_weight[0], in_weight[1], out_mine, out_other], axis=1)
    down_shard = down_weight.T
    other_tokens = swap_tensor(tokens)
    other_cotangent = swap_tensor(cotangent)
    attn_all = canonical(gather_blocks(attn_shard, order), order, mine)
    ffn_all = canonical(gather_blocks(ffn_shard, order), order, mine)
    down_all = canonical(gather_blocks(down_shard, order), order, mine)

    attn_joined = attn_all[:, : 3 * sub].reshape(dp, 3, sub, wide).transpose(1, 0, 2, 3)
    attn_joined = attn_joined.reshape(3, dp * sub, wide)
    gain_one = attn_all[:, 3 * sub, :sub].reshape(dp * sub).astype(jnp.float32)
    gain_two = attn_all[:, 3 * sub + 1, :sub].reshape(dp * sub).astype(jnp.float32)
    ffn_all = ffn_all.reshape(dp * sub, ffn_all.shape[2])
    in_act, in_lin = ffn_all[:, :units], ffn_all[:, units : 2 * units]
    out_t = ffn_all[:, 2 * units :]
    down_t = down_all.reshape(dp * sub, units)

    position, allowed = block_layout(block_seq, block_fill)
    turned = jnp.where(half == 0, 0, rows)
    position = jnp.roll(position, turned)
    allowed = jnp.roll(jnp.roll(allowed, turned, axis=0), turned, axis=1)
    cosine, sine_table = rope_tables(position)

    local_heads = wide // HD
    tokens_float = jnp.concatenate([tokens, other_tokens], axis=0).astype(jnp.float32)
    normed_one, inv_one = layer_stats(tokens_float)
    hidden_one = (normed_one * gain_one).astype(jnp.bfloat16)
    row_count = 2 * rows
    heads_shape = (row_count, local_heads, HD)
    projected = jnp.einsum(
        "rd,cde->cre", hidden_one, attn_joined, preferred_element_type=jnp.float32
    )
    queries = rope_apply(projected[0].reshape(heads_shape), cosine, sine_table).astype(jnp.bfloat16)
    key_heads = rope_apply(projected[1].reshape(heads_shape), cosine, sine_table).astype(
        jnp.bfloat16
    )
    values = projected[2].reshape(heads_shape).astype(jnp.bfloat16)
    mixed_heads, log_total = attend_forward(queries, key_heads, values, allowed)
    mixed_flat = mixed_heads.reshape(row_count, wide)
    swapped = swap_tensor(mixed_flat)
    swapped = jnp.concatenate([swapped[rows:], swapped[:rows]], axis=0)
    mixed_full = jnp.concatenate([mixed_flat, swapped], axis=1)
    resid_two = tokens_float + jnp.einsum(
        "rk,nk->rn", mixed_full, out_t, preferred_element_type=jnp.float32
    )
    normed_two, inv_two = layer_stats(resid_two)
    hidden_two = (normed_two * gain_two).astype(jnp.bfloat16)
    act_pre = jnp.dot(hidden_two, in_act, preferred_element_type=jnp.float32)
    linear = jnp.dot(hidden_two, in_lin, preferred_element_type=jnp.float32)
    gelu_value, gelu_slope = gelu_parts(act_pre)
    inner_act = (gelu_value * linear).astype(jnp.bfloat16)
    grad_rows = jnp.concatenate([cotangent, other_cotangent], axis=0)
    grad_inner = jnp.dot(grad_rows, down_t, preferred_element_type=jnp.float32)
    grad_act = (grad_inner * linear * gelu_slope).astype(jnp.bfloat16)
    grad_linear = (grad_inner * gelu_value).astype(jnp.bfloat16)
    part_two = jnp.dot(grad_act, in_act.T, preferred_element_type=jnp.float32) + jnp.dot(
        grad_linear, in_lin.T, preferred_element_type=jnp.float32
    )
    swapped = swap_tensor(part_two.astype(jnp.bfloat16)).astype(jnp.float32)
    grad_hidden_two = part_two + jnp.concatenate([swapped[rows:], swapped[:rows]], axis=0)
    down_out = jnp.einsum("rk,nk->rn", inner_act, down_t, preferred_element_type=jnp.float32)
    output = (
        resid_two[:rows]
        + down_out[:rows]
        + swap_tensor(down_out[rows:].astype(jnp.bfloat16)).astype(jnp.float32)
    ).astype(jnp.bfloat16)

    norm2_part = jnp.sum((grad_hidden_two * normed_two)[:rows], axis=0)
    grad_resid = grad_rows.astype(jnp.float32) + layer_back(
        grad_hidden_two * gain_two, normed_two, inv_two
    )
    resid_rows = grad_resid.astype(jnp.bfloat16)
    down_grad = jnp.dot(grad_rows.T, inner_act, preferred_element_type=jnp.float32)
    in_grad_act = jnp.dot(hidden_two.T, grad_act, preferred_element_type=jnp.float32)
    in_grad_lin = jnp.dot(hidden_two.T, grad_linear, preferred_element_type=jnp.float32)
    out_grad = jnp.dot(resid_rows.T, mixed_flat, preferred_element_type=jnp.float32)
    ffn_grads = jnp.concatenate([in_grad_act, in_grad_lin, out_grad, down_grad], axis=1)
    ffn_grads = scatter_sum(relative(ffn_grads.reshape(dp, sub, ffn_grads.shape[1]), mine))

    grad_mixed = (
        jnp.dot(resid_rows, out_t[:, :wide], preferred_element_type=jnp.float32)
        .astype(jnp.bfloat16)
        .reshape(heads_shape)
    )
    grad_query, grad_keys, grad_values = attend_backward(
        queries, key_heads, values, allowed, log_total, mixed_heads, grad_mixed
    )
    grad_joined = jnp.stack(
        [
            rope_back(grad_query, cosine, sine_table).reshape(row_count, wide),
            rope_back(grad_keys, cosine, sine_table).reshape(row_count, wide),
            grad_values.reshape(row_count, wide),
        ]
    ).astype(jnp.bfloat16)
    joined_grad = jnp.einsum(
        "rd,cre->cde", hidden_one, grad_joined, preferred_element_type=jnp.float32
    )
    joined_grad = joined_grad.reshape(3, dp, sub, wide).transpose(1, 0, 2, 3)
    joined_grad = scatter_sum(relative(joined_grad, mine))
    part_one = jnp.einsum(
        "cre,cde->rd", grad_joined, attn_joined, preferred_element_type=jnp.float32
    )
    grad_hidden_one = part_one[:rows] + swap_tensor(part_one[rows:].astype(jnp.bfloat16)).astype(
        jnp.float32
    )
    norm1_part = jnp.sum(grad_hidden_one * normed_one[:rows], axis=0)
    input_grad = (
        grad_resid[:rows]
        + layer_back(grad_hidden_one * gain_one, normed_one[:rows], inv_one[:rows])
    ).astype(jnp.bfloat16)
    norms = sum_all(jnp.stack([norm1_part, norm2_part]))
    norms = lax.dynamic_slice_in_dim(norms, mine * sub, sub, axis=1)
    in_grad = jnp.stack([ffn_grads[:, :units], ffn_grads[:, units : 2 * units]])
    return (
        output,
        input_grad,
        joined_grad,
        ffn_grads[:, 2 * units : 2 * units + wide].T,
        in_grad,
        ffn_grads[:, 2 * units + wide :].T,
        norms[0],
        norms[1],
    )


def solution(mesh):
    in_specs = (
        P(("dp", "tensor"), None),
        P(("dp", "tensor"), None),
        P("dp"),
        P("dp"),
        P(None, "dp", "tensor"),
        P("tensor", "dp"),
        P(None, "dp", "tensor"),
        P("tensor", "dp"),
        P("dp"),
        P("dp"),
    )
    out_specs = (
        P(("dp", "tensor"), None),
        P(("dp", "tensor"), None),
        P(None, "dp", "tensor"),
        P("tensor", "dp"),
        P(None, "dp", "tensor"),
        P("tensor", "dp"),
        P("dp"),
        P("dp"),
    )
    return jax.shard_map(local, mesh=mesh, in_specs=in_specs, out_specs=out_specs, check_vma=False)
```

```python
import functools
import math

import jax
import jax.numpy as jnp
from jax import lax
from jax.experimental import pallas as pl
from jax.experimental.pallas import tpu as pltpu
from jax.sharding import PartitionSpec as P

BLK = 128
HD = 64
LANES = 128
SUBLANES = 16

epsilon = 1e-05
rope_base = 160000.0
big_negative = -1e30


NT = (((1,), (1,)), ((), ()))
NN = (((1,), (0,)), ((), ()))
TN = (((0,), (0,)), ((), ()))


def mm(left, right, dims):
    return lax.dot_general(left, right, dims, preferred_element_type=jnp.float32)


def layer_stats(values):
    centre = values - jnp.mean(values, axis=-1, keepdims=True)
    inv_std = lax.rsqrt(jnp.mean(centre * centre, axis=-1, keepdims=True) + epsilon)
    return (centre * inv_std, inv_std)


def layer_back(grad_normed, normed, inv_std):
    mean_grad = jnp.mean(grad_normed, axis=-1, keepdims=True)
    mean_cross = jnp.mean(grad_normed * normed, axis=-1, keepdims=True)
    return inv_std * (grad_normed - mean_grad - normed * mean_cross)


def gelu_parts(values):
    normal_cdf = 0.5 * (1.0 + lax.erf(values * (1.0 / math.sqrt(2.0))))
    density = jnp.exp(-0.5 * values * values) * (1.0 / math.sqrt(2.0 * math.pi))
    return (values * normal_cdf, normal_cdf + values * density)


def swap_dp(values, mask):
    count = lax.axis_size("dp")
    return lax.ppermute(values, "dp", [(i, i ^ mask) for i in range(count)])


def swap_tensor(values):
    count = lax.axis_size("tensor")
    return lax.ppermute(values, "tensor", [(i, (i + 1) % count) for i in range(count)])


def gather_blocks(shard, bits):
    top = [1 << bit for bit in range(bits - 1, -1, -1)]
    masks = [0]
    for step in top[:2]:
        masks = masks + [mask | step for mask in masks]
    held = jnp.stack([shard] + [swap_dp(shard, mask) for mask in masks[1:]])
    for step in top[2:-2]:
        held = jnp.concatenate([held, swap_dp(held, step)], axis=0)
        masks = masks + [mask | step for mask in masks]
    pieces = [(held, masks)]
    for step in top[-2:]:
        pieces = pieces + [
            (swap_dp(array, step), [mask | step for mask in offsets]) for array, offsets in pieces
        ]
    return pieces


def gathered(shard, bits, mine):
    pieces = gather_blocks(shard, bits)
    if shard.shape[-2] % SUBLANES == 0:
        return [array for array, _ in pieces], [offsets for _, offsets in pieces]
    slots = sum((offsets for _, offsets in pieces), [])
    where = [0] * len(slots)
    for slot, block in enumerate(slots):
        where[block] = slot
    table = jnp.asarray(where, jnp.int32)[jnp.arange(len(slots), dtype=jnp.int32) ^ mine]
    blocks = jnp.take(jnp.concatenate([array for array, _ in pieces], axis=0), table, axis=0)
    blocks = jnp.moveaxis(blocks, 0, -3)
    joined = blocks.reshape(blocks.shape[:-3] + (-1, blocks.shape[-1]))
    return [joined[None]], [[0]]


def scatter_slots(keep, send):
    mask = 1
    while True:
        arrived = swap_dp(send, mask).astype(jnp.float32)
        count = keep.shape[0]
        if count == 1:
            return keep[0] + arrived[0]
        keep = keep.reshape((count // 2, 2) + keep.shape[1:])
        arrived = arrived.reshape(keep.shape)
        send = (keep[:, 1] + arrived[:, 1]).astype(jnp.bfloat16)
        keep = keep[:, 0] + arrived[:, 0]
        mask *= 2


def scatter_whole(blocks, mine):
    count = blocks.shape[0]
    slots = jnp.take(blocks, jnp.arange(count, dtype=jnp.int32) ^ mine, axis=0)
    pairs = slots.reshape((count // 2, 2) + blocks.shape[1:])
    return pairs[:, 0], pairs[:, 1].astype(jnp.bfloat16)


def sum_all(values):
    values = values + swap_tensor(values)
    mask = 1
    while mask < lax.axis_size("dp"):
        values = values + swap_dp(values, mask)
        mask *= 2
    return values


def put_blocks(mine, arrays, offsets, store):
    for array, masks in zip(arrays, offsets):
        for slot, mask in enumerate(masks):
            sub = array.shape[-2]
            first = 0 if masks == [0] and len(arrays) == 1 else pl.multiple_of((mine ^ mask) * sub, SUBLANES)
            store(pl.ds(first, sub), array, slot)


def first_half(shape):
    return lax.broadcasted_iota(jnp.int32, shape, len(shape) - 1) % LANES < HD


def turn(values):
    quarter = HD // 2
    lane = lax.broadcasted_iota(jnp.int32, values.shape, 1)
    ahead = pltpu.roll(values, LANES - quarter, 1)
    behind = pltpu.roll(values, quarter, 1)
    return jnp.where(lane % HD < quarter, ahead, behind)


def head_parts(tile):
    zero = jnp.zeros_like(tile)
    first = first_half(tile.shape)
    return (jnp.where(first, tile, zero), jnp.where(first, zero, tile))


def bias_rows(query_seq, key_seq):
    return jnp.where(query_seq[:, :1] == key_seq[:1, :], 0.0, big_negative)


def forward_kernel(setup, *refs):
    qkv_count, down_count = len(setup["qkv"]), len(setup["down"])
    mine_ref, tok_a, tok_b, cos_ref, sin_ref, qseq_ref, kseq_ref = refs[:7]
    qkv_refs = refs[7 : 7 + qkv_count]
    down_refs = refs[7 + qkv_count : 7 + qkv_count + down_count]
    rest = refs[7 + qkv_count + down_count :]
    mixed_ref, q_ref, k_ref, v_ref, hidden_ref, log_ref, gain_ref, w_ref, tail_ref = rest
    mine = mine_ref[0]
    rows = tok_a.shape[0]
    wide = q_ref.shape[1]

    def put_tail(where, array, slot):
        tail_ref[where, :] = array[slot]

    put_blocks(mine, down_refs, setup["down"], put_tail)
    pick_row = lax.broadcasted_iota(jnp.int32, (8, LANES), 0)
    pick_lane = lax.broadcasted_iota(jnp.int32, (8, LANES), 1)
    picks = jnp.where(pick_lane == setup["gain_lane"] + pick_row, 1.0, 0.0)
    picks = jnp.where(pick_row < 2, picks, 0.0).astype(jnp.bfloat16)
    gain_ref[...] = mm(picks, tail_ref[...], NT)

    def put_qkv(where, array, slot):
        for c in range(3):
            w_ref[c, where, :] = array[slot, c]

    put_blocks(mine, qkv_refs, setup["qkv"], put_qkv)
    gain = gain_ref[0:1, :]
    for part, tok in enumerate((tok_a, tok_b)):
        here = slice(part * rows, (part + 1) * rows)
        normed, _ = layer_stats(tok[...].astype(jnp.float32))
        hidden = (normed * gain).astype(jnp.bfloat16)
        hidden_ref[here, :] = hidden
        cosine, sine = cos_ref[here, :], sin_ref[here, :]
        for c, out in enumerate((q_ref, k_ref, v_ref)):
            projected = mm(hidden, w_ref[c], NN)
            if c == 2:
                out[here, :] = projected.astype(jnp.bfloat16)
                continue
            for tile in range(wide // LANES):
                lanes = slice(tile * LANES, (tile + 1) * LANES)
                piece = projected[:, lanes]
                piece = (piece * cosine + turn(piece) * sine).astype(jnp.bfloat16)
                if c == 0:
                    piece = piece * jnp.bfloat16(1.0 / math.sqrt(HD))
                out[here, lanes] = piece

    def chunk(step, carry):
        here = pl.ds(pl.multiple_of(step * BLK, BLK), BLK)
        bias = bias_rows(qseq_ref[here, :], kseq_ref[...])
        lane = lax.broadcasted_iota(jnp.int32, (BLK, LANES), 1)
        logs = jnp.zeros((BLK, LANES), jnp.float32)
        for tile in range(wide // LANES):
            lanes = slice(tile * LANES, (tile + 1) * LANES)
            keys = k_ref[:, lanes]
            total = jnp.zeros((BLK, LANES), jnp.float32)
            query_parts = head_parts(q_ref[here, lanes])
            value_parts = head_parts(v_ref[:, lanes])
            for side in range(2):
                scores = mm(query_parts[side], keys, NT) + bias
                peak = jnp.max(scores, axis=-1, keepdims=True)
                weights = jnp.exp(scores - peak)
                amount = jnp.sum(weights, axis=-1, keepdims=True)
                logs = jnp.where(lane == 2 * tile + side, peak + jnp.log(amount), logs)
                weights = (weights * (1.0 / amount)).astype(jnp.bfloat16)
                total = total + mm(weights, value_parts[side], NN)
            mixed_ref[here, lanes] = total.astype(jnp.bfloat16)
        log_ref[here, :] = logs
        return carry

    lax.fori_loop(0, 2 * rows // BLK, chunk, 0)


def middle_kernel(setup, *refs):
    ffn_count, down_count = len(setup["ffn"]), len(setup["down"])
    mine_ref, tok_a, tok_b, cot_a, cot_b, mixed_ref, mixed_other, gain_ref = refs[:8]
    ffn_refs = refs[8 : 8 + ffn_count]
    down_refs = refs[8 + ffn_count : 8 + ffn_count + down_count]
    rest = refs[8 + ffn_count + down_count :]
    send_ref, own_ref, resid_ref, hidden_ref, act_ref, lin_ref, inner_ref, out_ref, out_send = rest[:9]
    wout_mine, wa_ref, wl_ref, wd_ref, wout_other = rest[9:]
    mine = mine_ref[0]
    rows = tok_a.shape[0]
    wide = mixed_ref.shape[1]
    main, tail = setup["main"], setup["tail"]

    def put_ffn(where, array, slot):
        wa_ref[where, :main] = array[slot, :, :main]
        wl_ref[where, :main] = array[slot, :, main : 2 * main]
        wout_mine[where, :] = array[slot, :, 2 * main : 2 * main + wide]
        wout_other[where, :] = array[slot, :, 2 * main + wide : 2 * main + 2 * wide]
        ends = array[slot, :, 2 * main + 2 * wide :].astype(jnp.float32)
        inside = lax.broadcasted_iota(jnp.int32, ends.shape, 1) < tail
        wa_ref[where, main:] = jnp.where(inside, ends, 0.0).astype(jnp.bfloat16)
        turned = pltpu.roll(ends, LANES - tail, 1)
        wl_ref[where, main:] = jnp.where(inside, turned, 0.0).astype(jnp.bfloat16)

    def put_down(where, array, slot):
        wd_ref[where, :main] = array[slot, :, :main]
        ends = array[slot, :, main:]
        inside = lax.broadcasted_iota(jnp.int32, ends.shape, 1) < tail
        wd_ref[where, main:] = jnp.where(inside, ends, jnp.zeros_like(ends))

    put_blocks(mine, ffn_refs, setup["ffn"], put_ffn)
    put_blocks(mine, down_refs, setup["down"], put_down)
    gain = gain_ref[1:2, :]
    for part in range(2):
        here = slice(part * rows, (part + 1) * rows)
        there = slice((1 - part) * rows, (2 - part) * rows)
        tok, cot = ((tok_a, cot_a), (tok_b, cot_b))[part]
        resid = tok[...].astype(jnp.float32) + (
            mm(mixed_ref[here, :], wout_mine[...], NT) + mm(mixed_other[there, :], wout_other[...], NT)
        )
        resid_ref[here, :] = resid
        normed, _ = layer_stats(resid)
        hidden = (normed * gain).astype(jnp.bfloat16)
        hidden_ref[here, :] = hidden
        act_pre = mm(hidden, wa_ref[...], NN)
        linear = mm(hidden, wl_ref[...], NN)
        gelu_value, gelu_slope = gelu_parts(act_pre)
        grad_inner = mm(cot[...], wd_ref[...], NN)
        inner_ref[here, :] = (gelu_value * linear).astype(jnp.bfloat16)
        act_ref[here, :] = (grad_inner * linear * gelu_slope).astype(jnp.bfloat16)
        lin_ref[here, :] = (grad_inner * gelu_value).astype(jnp.bfloat16)
        total = mm(act_ref[here, :], wa_ref[...], NT) + mm(lin_ref[here, :], wl_ref[...], NT)
        own_ref[here, :] = total
        send_ref[here, :] = total.astype(jnp.bfloat16)
        down_out = mm(inner_ref[here, :], wd_ref[...], NT)
        if part == 0:
            out_ref[...] = resid + down_out
        else:
            out_send[...] = down_out.astype(jnp.bfloat16)


def ffn_grad_kernel(setup, *refs):
    mine_ref, cot_a, cot_b, hidden_ref, act_ref, lin_ref, inner_ref = refs[:7]
    keep_ref = refs[7]
    send_ref, total_ref = (refs[8], refs[9]) if setup["slots"] else (None, refs[8])
    mine = mine_ref[0]
    rows = cot_a.shape[0]
    main, tail = setup["main"], setup["tail"]
    act_grad = mm(hidden_ref[...], act_ref[...], TN)
    total_ref[:, :main] = act_grad[:, :main]
    ends = act_grad[:, main:]
    lin_grad = mm(hidden_ref[...], lin_ref[...], TN)
    total_ref[:, main : 2 * main] = lin_grad[:, :main]
    inside = lax.broadcasted_iota(jnp.int32, ends.shape, 1) < tail
    total_ref[:, 3 * main : 3 * main + LANES] = jnp.where(
        inside, ends, pltpu.roll(lin_grad[:, main:], tail, 1)
    )
    down_grad = mm(cot_a[...], inner_ref[:rows, :], TN) + mm(cot_b[...], inner_ref[rows:, :], TN)
    total_ref[:, 2 * main : 3 * main] = down_grad[:, :main]
    total_ref[:, 3 * main + LANES :] = down_grad[:, main:]
    write_slots(mine, total_ref, keep_ref, send_ref, setup)


def write_slots(mine, total_ref, keep_ref, send_ref, setup, index=()):
    if not setup["slots"]:
        keep_ref[index + (Ellipsis,)] = total_ref[...]
        return
    sub = setup["sub"]
    for slot in range(2 * keep_ref.shape[0]):
        first = pl.multiple_of((mine ^ slot) * sub, 8)
        block = total_ref[pl.ds(first, sub), :]
        if slot % 2 == 0:
            keep_ref[(slot // 2,) + index] = block
        else:
            send_ref[(slot // 2,) + index] = block.astype(jnp.bfloat16)


def backward_kernel(setup, *refs):
    qkv_count = len(setup["qkv"])
    mine_ref, tok_a, tok_b, cot_a, cot_b, own_ref, arrived_ref, resid_ref, gain_ref = refs[:9]
    q_ref, k_ref, v_ref, log_ref, mixed_ref, hidden_ref, wout_ref = refs[9:16]
    cos_ref, sin_ref, qseq_ref, kseq_ref = refs[16:20]
    qkv_refs = refs[20 : 20 + qkv_count]
    rest = refs[20 + qkv_count :]
    grad_ref, one_own, one_send, norm_ref, keep_ref = rest[:5]
    rest = rest[5:]
    send_ref = None
    if setup["slots"]:
        send_ref, rest = rest[0], rest[1:]
    w_ref, rows_ref, gm_ref, dq_ref, dk_ref, dv_ref, joined_ref, total_ref = rest
    mine = mine_ref[0]
    rows = tok_a.shape[0]
    wide = q_ref.shape[1]
    gain_one, gain_two = gain_ref[0:1, :], gain_ref[1:2, :]

    for part in range(2):
        here = slice(part * rows, (part + 1) * rows)
        there = slice((1 - part) * rows, (2 - part) * rows)
        cot = (cot_a, cot_b)[part]
        grad_hidden = own_ref[here, :] + arrived_ref[there, :].astype(jnp.float32)
        normed, inv_std = layer_stats(resid_ref[here, :])
        grad_resid = cot[...].astype(jnp.float32) + layer_back(grad_hidden * gain_two, normed, inv_std)
        if part == 0:
            norm_ref[1:2, :] = jnp.sum(grad_hidden * normed, axis=0, keepdims=True)
            grad_ref[...] = grad_resid
        rounded = grad_resid.astype(jnp.bfloat16)
        rows_ref[here, :] = rounded
        gm_ref[here, :] = mm(rounded, wout_ref[...], NN).astype(jnp.bfloat16)

    def put_qkv(where, array, slot):
        for c in range(3):
            w_ref[c, where, :] = array[slot, c]

    put_blocks(mine, qkv_refs, setup["qkv"], put_qkv)
    dk_ref[...] = jnp.zeros_like(dk_ref)
    dv_ref[...] = jnp.zeros_like(dv_ref)

    def chunk(step, carry):
        here = pl.ds(pl.multiple_of(step * BLK, BLK), BLK)
        bias = bias_rows(qseq_ref[here, :], kseq_ref[...])
        logs = log_ref[here, :]
        for tile in range(wide // LANES):
            lanes = slice(tile * LANES, (tile + 1) * LANES)
            keys, values = k_ref[:, lanes], v_ref[:, lanes]
            query_parts = head_parts(q_ref[here, lanes])
            grad_parts = head_parts(gm_ref[here, lanes])
            key_parts = head_parts(keys)
            mixed = mixed_ref[here, lanes].astype(jnp.float32)
            query_grad = jnp.zeros((BLK, LANES), jnp.float32)
            key_grad = jnp.zeros(keys.shape, jnp.float32)
            value_grad = jnp.zeros(keys.shape, jnp.float32)
            for side in range(2):
                head = 2 * tile + side
                grads = grad_parts[side]
                scores = mm(query_parts[side], keys, NT) + bias
                probs = jnp.exp(scores - logs[:, head : head + 1])
                value_grad = value_grad + mm(probs.astype(jnp.bfloat16), grads, TN)
                delta = jnp.sum(grads.astype(jnp.float32) * mixed, axis=-1, keepdims=True)
                grad_scores = (probs * (mm(grads, values, NT) - delta)).astype(jnp.bfloat16)
                query_grad = query_grad + mm(grad_scores, key_parts[side], NN)
                key_grad = key_grad + mm(grad_scores, query_parts[side], TN)
            dq_ref[here, lanes] = query_grad * (1.0 / math.sqrt(HD))
            dk_ref[:, lanes] += key_grad
            dv_ref[:, lanes] += value_grad
        return carry

    lax.fori_loop(0, 2 * rows // BLK, chunk, 0)
    for c, source in enumerate((dq_ref, dk_ref, dv_ref)):
        for tile in range(wide // LANES):
            lanes = slice(tile * LANES, (tile + 1) * LANES)
            piece = source[:, lanes]
            if c < 2:
                piece = piece * cos_ref[...] - turn(piece) * sin_ref[...]
            joined_ref[c, :, lanes] = piece.astype(jnp.bfloat16)
    total_ref[...] = mm(rows_ref[...], mixed_ref[...], TN)
    write_slots(mine, total_ref, keep_ref, send_ref, setup, (3,))
    for c in range(3):
        total_ref[...] = mm(hidden_ref[...], joined_ref[c], TN)
        write_slots(mine, total_ref, keep_ref, send_ref, setup, (c,))
    for part, tok in enumerate((tok_a, tok_b)):
        here = slice(part * rows, (part + 1) * rows)
        total = mm(joined_ref[0, here, :], w_ref[0], NT)
        total = total + mm(joined_ref[1, here, :], w_ref[1], NT)
        total = total + mm(joined_ref[2, here, :], w_ref[2], NT)
        normed, _ = layer_stats(tok[...].astype(jnp.float32))
        cross = jnp.sum(total * normed, axis=0, keepdims=True)
        if part == 0:
            norm_ref[0:1, :] = cross
            one_own[...] = total
        else:
            norm_ref[0:1, :] += cross
            one_send[...] = total.astype(jnp.bfloat16)


def last_kernel(tok_ref, grad_ref, own_ref, arrived_ref, gain_ref, out_ref):
    normed, inv_std = layer_stats(tok_ref[...].astype(jnp.float32))
    grads = own_ref[...] + arrived_ref[...].astype(jnp.float32)
    back = layer_back(grads * gain_ref[0:1, :], normed, inv_std)
    out_ref[...] = (grad_ref[...] + back).astype(jnp.bfloat16)


def call(kernel, name, mine, operands, outs, scratch, flops=0):
    specs, arrays = [], []
    for operand in operands:
        if isinstance(operand, tuple):
            array, block, index = operand
            specs.append(pl.BlockSpec(block, lambda i, index=index: index))
        else:
            array = operand
            specs.append(pl.BlockSpec(array.shape, lambda i, rank=array.ndim: (0,) * rank))
        arrays.append(array)
    head = [] if mine is None else [mine]
    head_specs = [] if mine is None else [pl.BlockSpec(memory_space=pltpu.SMEM)]
    size = sum(a.size * a.dtype.itemsize for a in arrays)
    return pl.pallas_call(
        kernel,
        name=name,
        grid=(1,),
        in_specs=head_specs + specs,
        out_specs=[pl.BlockSpec(o.shape, lambda i, rank=len(o.shape): (0,) * rank) for o in outs],
        out_shape=outs,
        scratch_shapes=scratch,
        compiler_params=pltpu.CompilerParams(vmem_limit_bytes=56 << 20),
        cost_estimate=pl.CostEstimate(flops=flops, bytes_accessed=size, transcendentals=0),
    )(*head, *arrays)


def block_layout(seq_ids, fill_counts):
    block_count = seq_ids.shape[0]
    block_order = jnp.arange(block_count, dtype=jnp.int32)
    same_seq = seq_ids[:, None] == seq_ids[None, :]
    first_block = jnp.min(jnp.where(same_seq, block_order[None, :], block_count), axis=1)
    return block_order - first_block


def local(
    tokens,
    cotangent,
    block_seq,
    block_fill,
    qkv_weight,
    out_weight,
    in_weight,
    down_weight,
    norm1_gain,
    norm2_gain,
):
    mine = lax.axis_index("dp")
    half = lax.axis_index("tensor")
    dp = lax.axis_size("dp")
    bits = dp.bit_length() - 1
    sub, wide = qkv_weight.shape[1:]
    units = in_weight.shape[2]
    rows, width = tokens.shape
    main, tail = units // LANES * LANES, units % LANES
    padded = main + LANES
    total_rows = 2 * rows
    slots = sub % SUBLANES == 0
    f32, bf16 = jnp.float32, jnp.bfloat16

    def shape(dims, dtype):
        return jax.ShapeDtypeStruct(dims, dtype)

    ends = jnp.zeros((sub, LANES - 2 * tail), bf16)
    out_mine = out_weight.T
    other_tokens = swap_tensor(tokens)
    out_other = swap_tensor(out_mine)
    down_shard = jnp.concatenate(
        [
            down_weight.T,
            norm1_gain[:, None],
            norm2_gain[:, None],
            jnp.zeros((sub, padded - units - 2), bf16),
        ],
        axis=1,
    )
    ffn_shard = jnp.concatenate(
        [
            in_weight[0, :, :main],
            in_weight[1, :, :main],
            out_mine,
            out_other,
            in_weight[0, :, main:],
            in_weight[1, :, main:],
            ends,
        ],
        axis=1,
    )
    down, down_at = gathered(down_shard, bits, mine)
    qkv, qkv_at = gathered(qkv_weight, bits, mine)
    ffn, ffn_at = gathered(ffn_shard, bits, mine)
    other_cotangent = swap_tensor(cotangent)
    block_mine = mine[None] if slots else jnp.zeros((1,), jnp.int32)

    half_blocks = rows // BLK
    turned = half * half_blocks
    first = jnp.roll(block_layout(block_seq, block_fill), -turned)
    seq_blocks = jnp.roll(block_seq, -turned)
    fill_blocks = jnp.roll(block_fill, -turned)
    offsets = jnp.arange(BLK, dtype=jnp.int32)
    position = (first[:, None] * BLK + offsets[None, :]).reshape(-1).astype(f32)
    seq_rows = jnp.repeat(seq_blocks, BLK)
    real = (offsets[None, :] < fill_blocks[:, None]).reshape(-1)
    query_seq = jnp.broadcast_to(seq_rows[:, None], (total_rows, LANES)).astype(f32)
    key_seq = jnp.broadcast_to(jnp.where(real, seq_rows, -1)[None], (8, total_rows)).astype(f32)
    quarter = HD // 2
    frequency = rope_base ** (-jnp.arange(quarter, dtype=f32) * (2.0 / HD))
    angles = position[:, None] * jnp.tile(frequency, LANES // quarter)[None, :]
    lane = jnp.arange(LANES)
    cosine = jnp.cos(angles)
    sine = jnp.sin(angles) * jnp.where(lane % HD < quarter, -1.0, 1.0)

    setup = {
        "qkv": qkv_at,
        "ffn": ffn_at,
        "down": down_at,
        "gain_lane": tail,
        "main": main,
        "tail": tail,
        "sub": sub,
        "slots": slots,
    }
    down_ends = [
        (array, array.shape[:-1] + (LANES,), (0,) * (array.ndim - 1) + (main // LANES,))
        for array in down
    ]
    mixed, queries, keys, values, hidden_one, logs, gains = call(
        functools.partial(forward_kernel, setup),
        "attention_forward",
        block_mine,
        [tokens, other_tokens, cosine, sine, query_seq, key_seq] + qkv + down_ends,
        [
            shape((total_rows, wide), bf16),
            shape((total_rows, wide), bf16),
            shape((total_rows, wide), bf16),
            shape((total_rows, wide), bf16),
            shape((total_rows, width), bf16),
            shape((total_rows, LANES), f32),
            shape((8, width), f32),
        ],
        [pltpu.VMEM((3, width, wide), bf16), pltpu.VMEM((width, LANES), bf16)],
        flops=8 * total_rows * width * wide,
    )
    mixed_other = swap_tensor(mixed)
    (
        two_send,
        two_own,
        resid_two,
        hidden_two,
        grad_act,
        grad_linear,
        inner_act,
        out_own,
        out_send,
        out_t,
    ) = call(
        functools.partial(middle_kernel, setup),
        "feed_forward",
        block_mine,
        [tokens, other_tokens, cotangent, other_cotangent, mixed, mixed_other, gains] + ffn + down,
        [
            shape((total_rows, width), bf16),
            shape((total_rows, width), f32),
            shape((total_rows, width), f32),
            shape((total_rows, width), bf16),
            shape((total_rows, padded), bf16),
            shape((total_rows, padded), bf16),
            shape((total_rows, padded), bf16),
            shape((rows, width), f32),
            shape((rows, width), bf16),
            shape((width, wide), bf16),
        ],
        [
            pltpu.VMEM((width, padded), bf16),
            pltpu.VMEM((width, padded), bf16),
            pltpu.VMEM((width, padded), bf16),
            pltpu.VMEM((width, wide), bf16),
        ],
        flops=16 * total_rows * width * units,
    )
    two_other = swap_tensor(two_send)
    out_other_rows = swap_tensor(out_send)
    output = (out_own + out_other_rows.astype(f32)).astype(bf16)

    def slot_shapes(*dims):
        if slots:
            return [shape((dp // 2,) + dims, f32), shape((dp // 2,) + dims, bf16)]
        return [shape(dims[:-2] + (width, dims[-1]), f32)]

    def scattered(results):
        if slots:
            return scatter_slots(*results)
        (whole,) = results
        blocks = whole.reshape(whole.shape[:-2] + (dp, sub, whole.shape[-1]))
        return scatter_slots(*scatter_whole(jnp.moveaxis(blocks, -3, 0), mine))

    ffn_width = 3 * main + 2 * LANES
    ffn_slots = call(
        functools.partial(ffn_grad_kernel, setup),
        "feed_forward_grads",
        block_mine,
        [cotangent, other_cotangent, hidden_two, grad_act, grad_linear, inner_act],
        slot_shapes(sub, ffn_width),
        [pltpu.VMEM((width, ffn_width), f32)],
        flops=6 * total_rows * width * units,
    )
    ffn_grads = scattered(ffn_slots)

    results = call(
        functools.partial(backward_kernel, setup),
        "attention_backward",
        block_mine,
        [
            tokens,
            other_tokens,
            cotangent,
            other_cotangent,
            two_own,
            two_other,
            resid_two,
            gains,
            queries,
            keys,
            values,
            logs,
            mixed,
            hidden_one,
            out_t,
            cosine,
            sine,
            query_seq,
            key_seq,
        ]
        + qkv,
        [
            shape((rows, width), f32),
            shape((rows, width), f32),
            shape((rows, width), bf16),
            shape((8, width), f32),
        ]
        + slot_shapes(4, sub, wide),
        [
            pltpu.VMEM((3, width, wide), bf16),
            pltpu.VMEM((total_rows, width), bf16),
            pltpu.VMEM((total_rows, wide), bf16),
            pltpu.VMEM((total_rows, wide), f32),
            pltpu.VMEM((total_rows, wide), f32),
            pltpu.VMEM((total_rows, wide), f32),
            pltpu.VMEM((3, total_rows, wide), bf16),
            pltpu.VMEM((width, wide), f32),
        ],
        flops=16 * total_rows * width * wide,
    )
    grad_resid, one_own, one_send, norm_parts = results[:4]
    one_other = swap_tensor(one_send)
    norms = sum_all(norm_parts[:2])
    attn_grads = scattered(results[4:])
    (input_grad,) = call(
        last_kernel,
        "input_grad",
        None,
        [tokens, grad_resid, one_own, one_other, gains],
        [shape((rows, width), bf16)],
        [],
    )
    norms = lax.dynamic_slice_in_dim(norms, mine * sub, sub, axis=1)
    act_grad = jnp.concatenate(
        [ffn_grads[:, :main], ffn_grads[:, 3 * main : 3 * main + tail]], axis=1
    )
    lin_grad = jnp.concatenate(
        [ffn_grads[:, main : 2 * main], ffn_grads[:, 3 * main + tail : 3 * main + 2 * tail]], axis=1
    )
    down_grad = jnp.concatenate(
        [ffn_grads[:, 2 * main : 3 * main], ffn_grads[:, 3 * main + LANES :][:, :tail]], axis=1
    )
    return (
        output,
        input_grad,
        attn_grads[:3],
        attn_grads[3].T,
        jnp.stack([act_grad, lin_grad]),
        down_grad.T,
        norms[0],
        norms[1],
    )


def solution(mesh):
    in_specs = (
        P(("dp", "tensor"), None),
        P(("dp", "tensor"), None),
        P("dp"),
        P("dp"),
        P(None, "dp", "tensor"),
        P("tensor", "dp"),
        P(None, "dp", "tensor"),
        P("tensor", "dp"),
        P("dp"),
        P("dp"),
    )
    out_specs = (
        P(("dp", "tensor"), None),
        P(("dp", "tensor"), None),
        P(None, "dp", "tensor"),
        P("tensor", "dp"),
        P(None, "dp", "tensor"),
        P("tensor", "dp"),
        P("dp"),
        P("dp"),
    )
    return jax.shard_map(local, mesh=mesh, in_specs=in_specs, out_specs=out_specs, check_vma=False)
```
